256 devices in a mesh: seq: 64 (over z_hi, x, y), head: 4 (over z_lo, core).
Axes of the slice: x: 4, y: 4, z: 8 (z_hi: 4, z_lo: 2; z = z_hi * 2 + z_lo), core: 2. Of those that a mesh axis runs over, the one named last changes fastest.
Arguments:
- q_tokens: bfloat16 [16384, 4096], P(('seq', 'head')), may hold values from -6 to 6
- k_tokens: bfloat16 [16384, 4096], P(('seq', 'head')), may hold values from -6 to 6
- v_tokens: bfloat16 [16384, 4096], P(('seq', 'head')), may hold values from -4 to 4
- grad_out: bfloat16 [16384, 4096], P(('seq', 'head')), may hold values from -4 to 4
- block_lists: int32 [256, 3], P('seq'), may hold values from 0 to 3, as said below
- block_valid: int32 [256, 3], P('seq'), may hold values from 0 to 1, as said below
Outputs:
- attended: bfloat16 [16384, 4096], P(('seq', 'head'))
- grad_q: bfloat16 [16384, 4096], P('seq', 'head')
- grad_k: bfloat16 [16384, 4096], P('seq', 'head')
- grad_v: bfloat16 [16384, 4096], P('seq', 'head')
The draws below stay inside these ranges and needn't reach their ends.
Inputs may be any that keep to these rules, and one draw needn't show every extreme that they name: `block_lists`: among the 4 entries of one level of the query blocks of one span of 256 tokens, exactly 2 distinct values appear. `block_valid`: entry e of query block b is 0 wherever b // 4 < 2 * 4^e.
All inputs are finite; a program needn't handle non-finite values.
Results may differ from the reference program's by a relative error of at most 0.022.
Values may be sent and summed in bfloat16 or wider, within the bound.
No kernel may reach another device: no remote copies, remote signals or barrier semaphores. Data moves between devices by JAX's collectives and lax.ppermute only.
A program may use at most 128 MiB of HBM per device.

```python
import jax
import jax.numpy as jnp
from jax import lax

HEADS = 32
HEAD_DIM = 128
TOK_DEV = 256
WINDOW = 256
BLOCK = 64
LEVELS = 3
TOKENS = 16384
QB_DEV = 4
USED = 2
QBLOCKS = 256


def draw_q_tokens(key, part):
    sub = jax.random.fold_in(key, 1)
    return jnp.clip(jax.random.normal(sub, (TOKENS, HEADS * HEAD_DIM), jnp.float32), -4.0, 4.0).astype(jnp.bfloat16)


def draw_k_tokens(key, part):
    sub = jax.random.fold_in(key, 2)
    return jnp.clip(jax.random.normal(sub, (TOKENS, HEADS * HEAD_DIM), jnp.float32), -4.0, 4.0).astype(jnp.bfloat16)


def draw_block_lists(key, part):
    span_count = TOKENS // TOK_DEV
    subkeys = jax.random.split(jax.random.fold_in(key, 11), span_count * LEVELS)

    def one_group(subkey):
        first_key, second_key, third_key = jax.random.split(subkey, 3)
        chosen = jax.random.permutation(first_key, QB_DEV)[:USED]
        extra = jax.random.randint(second_key, (QB_DEV,), 0, USED)
        order_ids = jnp.arange(QB_DEV, dtype=jnp.int32)
        slot_ids = jnp.where(order_ids < USED, order_ids, extra)
        slot_ids = jax.random.permutation(third_key, slot_ids)
        return chosen[slot_ids]
    table = jax.vmap(one_group)(subkeys)
    table = table.reshape(span_count, LEVELS, QB_DEV).transpose(0, 2, 1).reshape(QBLOCKS, LEVELS)
    return table.astype(jnp.int32)


def draw_block_valid(key, part):
    spans = jnp.arange(QBLOCKS, dtype=jnp.int32)[:, None] // QB_DEV
    reach = 2 * 4 ** jnp.arange(LEVELS, dtype=jnp.int32)[None, :]
    coins = jax.random.randint(jax.random.fold_in(key, 13), (QBLOCKS, LEVELS), 0, 4)
    return ((spans >= reach) & (coins > 0)).astype(jnp.int32)


def steps_of(key, shape, shards, least, top_value):
    def one(axis_at, blocks):
        steps = jax.random.uniform(jax.random.fold_in(jax.random.fold_in(key, 6), axis_at), (blocks,), jnp.float32, least / len(shards), top_value / len(shards))
        return jnp.repeat(jnp.exp(steps), shape[axis_at] // blocks).reshape((-1,) + (1,) * (len(shape) - axis_at - 1))

    level = one(*shards[0])
    for cut in shards[1:]:
        level = level * one(*cut)
    return level


def normal_values(key, shape, spread, most, cuts=(), held_as=jnp.bfloat16):
    level = steps_of(key, shape, cuts, -0.22, 0.18) if cuts else 1.0
    values = jax.random.normal(key, shape, jnp.float32) * spread * level
    return jnp.minimum(jnp.maximum(values, -most), most).astype(held_as)


def setup_inputs(seed: int = 0) -> dict:
    seeds = jax.random.split(jax.random.key(seed), 7)
    q_tokens = draw_q_tokens(jax.random.fold_in(seeds[6], 71), 0)
    k_tokens = draw_k_tokens(jax.random.fold_in(seeds[6], 71), 0)
    v_tokens = normal_values(seeds[2], (TOKENS, HEADS * HEAD_DIM), 1.0, 4.0, ((0, 256),))
    grad_out = normal_values(seeds[3], (TOKENS, HEADS * HEAD_DIM), 1.0, 4.0, ((0, 256),))
    block_lists = draw_block_lists(jax.random.fold_in(seeds[6], 71), 0)
    block_valid = draw_block_valid(jax.random.fold_in(seeds[6], 71), 0)
    return dict(q_tokens=q_tokens, k_tokens=k_tokens, v_tokens=v_tokens, grad_out=grad_out, block_lists=block_lists, block_valid=block_valid)


NEG = -1.0e30


def rounded(values_in):
    return lax.optimization_barrier(values_in.astype(jnp.bfloat16)).astype(jnp.float32)


def reference(q_tokens, k_tokens, v_tokens, grad_out, block_lists, block_valid):
    feature_cols = HEADS * HEAD_DIM
    score_scale = HEAD_DIM ** -0.5
    span_count = TOKENS // TOK_DEV
    zero_rows = jnp.zeros((WINDOW, feature_cols), k_tokens.dtype)
    key_padded = jnp.concatenate([zero_rows, k_tokens], 0)
    value_padded = jnp.concatenate([zero_rows, v_tokens], 0)
    key_blocks = k_tokens.reshape(QBLOCKS, BLOCK, feature_cols)
    value_blocks = v_tokens.reshape(QBLOCKS, BLOCK, feature_cols)
    reach_spans = 2 * 4 ** jnp.arange(LEVELS, dtype=jnp.int32)
    inner_rows = jnp.arange(BLOCK, dtype=jnp.int32)

    def one_span(carry, span_index):
        acc_k, acc_v = carry
        start = span_index * TOK_DEV
        query_f = lax.dynamic_slice_in_dim(q_tokens, start, TOK_DEV, 0).astype(jnp.float32).reshape(TOK_DEV, HEADS, HEAD_DIM)
        cotan_f = lax.dynamic_slice_in_dim(grad_out, start, TOK_DEV, 0).astype(jnp.float32).reshape(TOK_DEV, HEADS, HEAD_DIM)
        key_win = lax.dynamic_slice_in_dim(key_padded, start, WINDOW + TOK_DEV, 0).astype(jnp.float32).reshape(WINDOW + TOK_DEV, HEADS, HEAD_DIM)
        value_win = lax.dynamic_slice_in_dim(value_padded, start, WINDOW + TOK_DEV, 0).astype(jnp.float32).reshape(WINDOW + TOK_DEV, HEADS, HEAD_DIM)
        picks = lax.dynamic_slice_in_dim(block_lists, span_index * QB_DEV, QB_DEV, 0)
        valid_rows = lax.dynamic_slice_in_dim(block_valid, span_index * QB_DEV, QB_DEV, 0)
        target = jnp.clip((span_index - reach_spans)[None, :] * QB_DEV + picks, 0, QBLOCKS - 1).astype(jnp.int32)
        key_far = key_blocks[target].astype(jnp.float32).reshape(QB_DEV, LEVELS * BLOCK, HEADS, HEAD_DIM)
        value_far = value_blocks[target].astype(jnp.float32).reshape(QB_DEV, LEVELS * BLOCK, HEADS, HEAD_DIM)
        query_pos = start + jnp.arange(TOK_DEV, dtype=jnp.int32)
        key_pos = start - WINDOW + jnp.arange(WINDOW + TOK_DEV, dtype=jnp.int32)
        near_mask = (key_pos[None, :] <= query_pos[:, None]) & (key_pos[None, :] > query_pos[:, None] - WINDOW) & (key_pos[None, :] >= 0)
        score_win = jnp.einsum('thd,jhd->htj', query_f, key_win) * score_scale
        score_win = jnp.where(near_mask[None], score_win, NEG)
        query_blk = query_f.reshape(QB_DEV, BLOCK, HEADS, HEAD_DIM)
        cotan_blk = cotan_f.reshape(QB_DEV, BLOCK, HEADS, HEAD_DIM)
        far_mask = jnp.repeat(valid_rows > 0, BLOCK, axis=1)
        score_far = jnp.einsum('bqhd,bkhd->hbqk', query_blk, key_far) * score_scale
        score_far = jnp.where(far_mask[None, :, None, :], score_far, NEG)
        row_top = jnp.maximum(jnp.max(score_win, -1), jnp.max(score_far, -1).reshape(HEADS, TOK_DEV))
        row_total = jnp.sum(jnp.exp(score_win - row_top[..., None]), -1)
        row_total = row_total + jnp.sum(jnp.exp(score_far - row_top.reshape(HEADS, QB_DEV, BLOCK)[..., None]), -1).reshape(HEADS, TOK_DEV)
        log_total = row_top + jnp.log(row_total)
        weight_win = jnp.exp(score_win - log_total[..., None])
        weight_far = jnp.exp(score_far - log_total.reshape(HEADS, QB_DEV, BLOCK)[..., None])
        weight_win_b = rounded(weight_win)
        weight_far_b = rounded(weight_far)
        attended_f = jnp.einsum('htj,jhd->thd', weight_win_b, value_win)
        attended_f = attended_f + jnp.einsum('hbqk,bkhd->bqhd', weight_far_b, value_far).reshape(TOK_DEV, HEADS, HEAD_DIM)
        attended_b = rounded(attended_f)
        delta = jnp.einsum('thd,thd->ht', cotan_f, attended_b)
        dscore_win = weight_win * (jnp.einsum('thd,jhd->htj', cotan_f, value_win) - delta[..., None])
        dscore_far = weight_far * (jnp.einsum('bqhd,bkhd->hbqk', cotan_blk, value_far) - delta.reshape(HEADS, QB_DEV, BLOCK)[..., None])
        dscore_win_b = rounded(dscore_win)
        dscore_far_b = rounded(dscore_far)
        query_grad = jnp.einsum('htj,jhd->thd', dscore_win_b, key_win)
        query_grad = query_grad + jnp.einsum('hbqk,bkhd->bqhd', dscore_far_b, key_far).reshape(TOK_DEV, HEADS, HEAD_DIM)
        query_grad = score_scale * query_grad
        key_grad_win = (score_scale * jnp.einsum('htj,thd->jhd', dscore_win_b, query_f)).reshape(WINDOW + TOK_DEV, feature_cols)
        value_grad_win = jnp.einsum('htj,thd->jhd', weight_win_b, cotan_f).reshape(WINDOW + TOK_DEV, feature_cols)
        key_grad_far = (score_scale * jnp.einsum('hbqk,bqhd->bkhd', dscore_far_b, query_blk)).reshape(-1, feature_cols)
        value_grad_far = jnp.einsum('hbqk,bqhd->bkhd', weight_far_b, cotan_blk).reshape(-1, feature_cols)
        acc_k = lax.dynamic_update_slice_in_dim(acc_k, lax.dynamic_slice_in_dim(acc_k, start, WINDOW + TOK_DEV, 0) + key_grad_win, start, 0)
        acc_v = lax.dynamic_update_slice_in_dim(acc_v, lax.dynamic_slice_in_dim(acc_v, start, WINDOW + TOK_DEV, 0) + value_grad_win, start, 0)
        far_rows = (WINDOW + target[:, :, None] * BLOCK + inner_rows[None, None, :]).reshape(-1).astype(jnp.int32)
        acc_k = acc_k.at[far_rows].add(key_grad_far)
        acc_v = acc_v.at[far_rows].add(value_grad_far)
        attended_rows = attended_b.reshape(TOK_DEV, feature_cols).astype(jnp.bfloat16)
        query_rows = query_grad.reshape(TOK_DEV, feature_cols).astype(jnp.bfloat16)
        return (acc_k, acc_v), (attended_rows, query_rows)

    start_acc = jnp.zeros((WINDOW + TOKENS, feature_cols), jnp.float32)
    (acc_k, acc_v), (attended_all, query_all) = lax.scan(one_span, (start_acc, start_acc), jnp.arange(span_count, dtype=jnp.int32))
    attended = attended_all.reshape(TOKENS, feature_cols)
    grad_q = query_all.reshape(TOKENS, feature_cols)
    grad_k = acc_k[WINDOW:].astype(jnp.bfloat16)
    grad_v = acc_v[WINDOW:].astype(jnp.bfloat16)
    return (attended, grad_q, grad_k, grad_v)
```

```python
import jax
import jax.numpy as jnp
from jax import lax
from jax.experimental import pallas as pl
from jax.experimental.pallas import tpu as pltpu
from jax.sharding import PartitionSpec as P

HEAD_DIM = 128
WINDOW = 256
BLOCK = 64
LEVELS = 3
NEG = -1e30


def passed_along(shard, by):
    peers = lax.axis_size("seq")
    pairs = [(i, i + by) for i in range(peers) if 0 <= i + by < peers]
    return lax.ppermute(shard, "seq", pairs)


def pack_body(a_ref, b_ref, out_ref):
    out_ref[0, 0] = a_ref[...]
    out_ref[0, 1] = b_ref[...]


def pack_pair(a, b, parts):
    rows, cols = a.shape
    piece = pl.BlockSpec((rows, cols // parts), lambda i: (0, i))
    return pl.pallas_call(
        pack_body,
        out_shape=jax.ShapeDtypeStruct((parts, 2, rows, cols // parts), a.dtype),
        grid=(parts,),
        in_specs=[piece, piece],
        out_specs=pl.BlockSpec((1, 2, rows, cols // parts), lambda i: (i, 0, 0, 0)),
        name="pack_pair",
    )(a, b)


def pick_body(idx_ref, kv_ref, *rest):
    outs, sems = rest[:-1], rest[-1]
    copies = []
    for level in reversed(range(LEVELS)):
        for slot in range(2):
            copies.append(
                pltpu.make_async_copy(
                    kv_ref.at[idx_ref[level, slot]], outs[level].at[slot], sems.at[level, slot]
                )
            )
    for copy in copies:
        copy.start()
    for copy in copies:
        copy.wait()


def pick_blocks(idx, kv):
    shape = jax.ShapeDtypeStruct((2,) + kv.shape[1:], kv.dtype)
    return pl.pallas_call(
        pick_body,
        out_shape=[shape] * LEVELS,
        grid_spec=pltpu.PrefetchScalarGridSpec(
            num_scalar_prefetch=1,
            in_specs=[pl.BlockSpec(memory_space=pltpu.VMEM)],
            out_specs=[pl.BlockSpec(memory_space=pl.ANY)] * LEVELS,
            grid=(1,),
            scratch_shapes=[pltpu.SemaphoreType.DMA((LEVELS, 2))],
        ),
        name="pick_blocks",
    )(idx, kv)


def dot_nt(a, b):
    return lax.dot_general(a, b, (((1,), (1,)), ((), ())), preferred_element_type=jnp.float32)


def dot_nn(a, b):
    return lax.dot_general(a, b, (((1,), (0,)), ((), ())), preferred_element_type=jnp.float32)


def dot_tn(a, b):
    return lax.dot_general(a, b, (((0,), (0,)), ((), ())), preferred_element_type=jnp.float32)


def attend_body(
    span_ref, lists_ref, valid_ref, used_ref,
    qd_ref, own_ref, prev_ref, far0_ref, far1_ref, far2_ref,
    att_ref, gq_ref, gown_ref, gprev_ref, gfar0_ref, gfar1_ref, gfar2_ref,
    bias_ref, k_ref, v_ref,
):
    rows = 4 * BLOCK
    near = WINDOW + rows
    scale = HEAD_DIM ** -0.5

    @pl.when(pl.program_id(0) == 0)
    def _():
        first = span_ref[0] == 0
        i = lax.broadcasted_iota(jnp.int32, (rows, near), 0)
        j = lax.broadcasted_iota(jnp.int32, (rows, near), 1)
        low = jnp.where(first, WINDOW, 0)
        ok = (j > i) & (j <= i + WINDOW) & (j >= low)
        bias_ref[:, :near] = jnp.where(ok, 0.0, NEG)
        for b in range(4):
            for level in range(LEVELS):
                for slot in range(2):
                    hit = (valid_ref[b, level] > 0) & (lists_ref[b, level] == used_ref[level, slot])
                    value = jnp.where(hit, 0.0, NEG)
                    at = near + (level * 2 + slot) * BLOCK
                    bias_ref[b * BLOCK:(b + 1) * BLOCK, at:at + BLOCK] = jnp.full(
                        (BLOCK, BLOCK), value, jnp.float32
                    )

    at = 0
    for ref, blocks in ((prev_ref, 4), (own_ref, 4), (far0_ref, 2), (far1_ref, 2), (far2_ref, 2)):
        for b in range(blocks):
            k_ref[at:at + BLOCK, :] = ref[b, 0]
            v_ref[at:at + BLOCK, :] = ref[b, 1]
            at += BLOCK
    q = qd_ref[:, 0].reshape(rows, HEAD_DIM)
    d = qd_ref[:, 1].reshape(rows, HEAD_DIM)
    s = dot_nt(q, k_ref[...]) * scale + bias_ref[...]
    m = jnp.max(s, -1, keepdims=True)
    p = jnp.exp(s - m)
    total = jnp.sum(p, -1, keepdims=True)
    w = p * (1.0 / total)
    wb = w.astype(jnp.bfloat16)
    att = dot_nn(wb, v_ref[...]).astype(jnp.bfloat16)
    att_ref[...] = att.reshape(4, BLOCK, HEAD_DIM)
    delta = jnp.sum(d.astype(jnp.float32) * att.astype(jnp.float32), -1, keepdims=True)
    dp = dot_nt(d, v_ref[...])
    ds = (w * (dp - delta)).astype(jnp.bfloat16)
    gq_ref[...] = (dot_nn(ds, k_ref[...]) * scale).astype(jnp.bfloat16)
    gk = dot_tn(ds, q) * scale
    gv = dot_tn(wb, d)
    gown_ref[0] = gk[WINDOW:near]
    gown_ref[1] = gv[WINDOW:near]
    gprev_ref[:, 0] = gk[:WINDOW].astype(jnp.bfloat16).reshape(4, BLOCK, HEAD_DIM)
    gprev_ref[:, 1] = gv[:WINDOW].astype(jnp.bfloat16).reshape(4, BLOCK, HEAD_DIM)
    for level, ref in enumerate((gfar0_ref, gfar1_ref, gfar2_ref)):
        a = near + level * 2 * BLOCK
        ref[:, 0] = gk[a:a + 2 * BLOCK].astype(jnp.bfloat16).reshape(2, BLOCK, HEAD_DIM)
        ref[:, 1] = gv[a:a + 2 * BLOCK].astype(jnp.bfloat16).reshape(2, BLOCK, HEAD_DIM)


def attend(span, lists, valid, used, qd, own, prev, fars):
    cols = qd.shape[-1]
    heads = cols // HEAD_DIM
    rows = 4 * BLOCK
    keys = WINDOW + rows + 2 * LEVELS * BLOCK

    def piece(*lead):
        return pl.BlockSpec(lead + (HEAD_DIM,), lambda h, *_: (0,) * len(lead) + (h,))

    four, two = piece(4, 2, BLOCK), piece(2, 2, BLOCK)
    bf = jnp.bfloat16
    return pl.pallas_call(
        attend_body,
        out_shape=[
            jax.ShapeDtypeStruct((4, BLOCK, cols), bf),
            jax.ShapeDtypeStruct((rows, cols), bf),
            jax.ShapeDtypeStruct((2, rows, cols), jnp.float32),
            jax.ShapeDtypeStruct((4, 2, BLOCK, cols), bf),
        ] + [jax.ShapeDtypeStruct((2, 2, BLOCK, cols), bf)] * LEVELS,
        grid_spec=pltpu.PrefetchScalarGridSpec(
            num_scalar_prefetch=4,
            grid=(heads,),
            in_specs=[four, four, four, two, two, two],
            out_specs=[piece(4, BLOCK), piece(rows), piece(2, rows), four, two, two, two],
            scratch_shapes=[
                pltpu.VMEM((rows, keys), jnp.float32),
                pltpu.VMEM((keys, HEAD_DIM), bf),
                pltpu.VMEM((keys, HEAD_DIM), bf),
            ],
        ),
        name="attend",
    )(span, lists, valid, used, qd, own, prev, *fars)


def total_body(idx_ref, gown_ref, gprev_ref, gfar0_ref, gfar1_ref, gfar2_ref, gk_ref, gv_ref, acc_ref):
    for b in range(4):
        for which in range(2):
            acc_ref[b, which] = gown_ref[which, b * BLOCK:(b + 1) * BLOCK] + gprev_ref[b, which].astype(jnp.float32)
    for level, ref in enumerate((gfar0_ref, gfar1_ref, gfar2_ref)):
        for slot in range(2):
            at = idx_ref[level, slot]
            acc_ref[at] += ref[slot].astype(jnp.float32)
    for b in range(4):
        gk_ref[b * BLOCK:(b + 1) * BLOCK, :] = acc_ref[b, 0].astype(jnp.bfloat16)
        gv_ref[b * BLOCK:(b + 1) * BLOCK, :] = acc_ref[b, 1].astype(jnp.bfloat16)


def total(idx, gown, gprev, gfars):
    cols = gown.shape[-1]
    rows = 4 * BLOCK
    step = 256

    def piece(*lead):
        return pl.BlockSpec(lead + (step,), lambda h, *_: (0,) * len(lead) + (h,))

    out = jax.ShapeDtypeStruct((rows, cols), jnp.bfloat16)
    return pl.pallas_call(
        total_body,
        out_shape=[out, out],
        grid_spec=pltpu.PrefetchScalarGridSpec(
            num_scalar_prefetch=1,
            grid=(cols // step,),
            in_specs=[piece(2, rows), piece(4, 2, BLOCK)] + [piece(2, 2, BLOCK)] * LEVELS,
            out_specs=[piece(rows), piece(rows)],
            scratch_shapes=[pltpu.VMEM((4, 2, BLOCK, step), jnp.float32)],
        ),
        name="total",
    )(idx, gown, gprev, *gfars)


def spread(x):
    return lax.all_to_all(x, "head", split_axis=0, concat_axis=0)


def per_device(q_tokens, k_tokens, v_tokens, grad_out, block_lists, block_valid):
    parts = lax.axis_size("head")
    span = lax.axis_index("seq").astype(jnp.int32).reshape(1)
    used = jnp.stack([jnp.min(block_lists, 0), jnp.max(block_lists, 0)], 1)
    asked = jnp.stack([passed_along(used[level], -2 * 4**level) for level in range(LEVELS)])
    own = spread(pack_pair(k_tokens, v_tokens, parts))
    picked = pick_blocks(asked, own)
    fars = [None] * LEVELS
    for level in reversed(range(LEVELS)):
        fars[level] = passed_along(picked[level], 2 * 4**level)
    prev = passed_along(own, 1)
    qd = spread(pack_pair(q_tokens, grad_out, parts))
    att, grad_q, gown, gprev, *gfars = attend(
        span, block_lists, block_valid, used, qd, own, prev, fars
    )
    back = [None] * LEVELS
    for level in reversed(range(LEVELS)):
        back[level] = passed_along(gfars[level], -2 * 4**level)
    back_prev = passed_along(gprev, -1)
    attended = spread(att).transpose(1, 0, 2).reshape(q_tokens.shape)
    grad_k, grad_v = total(asked, gown, back_prev, back)
    return attended, grad_q, grad_k, grad_v


def solution(mesh):
    tokens = P(("seq", "head"), None)
    return jax.shard_map(
        per_device,
        mesh=mesh,
        in_specs=(tokens,) * 4 + (P("seq", None),) * 2,
        out_specs=(tokens,) + (P("seq", "head"),) * 3,
        check_vma=False,
    )
```

```python
import functools

import jax
import jax.numpy as jnp
from jax import lax
from jax.experimental import pallas as pl
from jax.experimental.pallas import tpu as pltpu
from jax.sharding import PartitionSpec as P

HEAD_DIM = 128
WINDOW = 256
BLOCK = 64
LEVELS = 3
NEG = -1e30


DETOURS = {1: {15: 0}, 2: {15: 1}, 8: {14: 6, 15: 7}}
PLANE = 16


def pairs_of(peers, by, detour):
    pairs = []
    for i in range(peers):
        if i + by < peers:
            to = i + by
            if detour and to // PLANE > i // PLANE:
                at = DETOURS[by].get(i % PLANE)
                to = to if at is None else i // PLANE * PLANE + at
            pairs.append((i, to))
    return pairs


def passed(shard, by, detour=False):
    peers = lax.axis_size("seq")
    pairs = pairs_of(peers, abs(by), detour)
    if by < 0:
        pairs = [(peers - 1 - i, peers - 1 - j) for i, j in pairs]
    return lax.ppermute(shard, "seq", pairs)


def stepped(shard, sign):
    peers = lax.axis_size("seq")
    relays = [at for table in DETOURS.values() for at in table.values()]
    pairs = [(i, i + PLANE) for i in range(peers - PLANE) if i % PLANE in relays]
    if sign < 0:
        pairs = [(peers - 1 - i, peers - 1 - j) for i, j in pairs]
    return lax.ppermute(shard, "seq", pairs)


def relayed(first, second, third, sign):
    peers = lax.axis_size("seq")
    at = lax.axis_index("seq")
    at = at if sign > 0 else peers - 1 - at
    here = at % PLANE
    hits = [
        functools.reduce(jnp.logical_or, [here == v for v in DETOURS[by].values()]) for by in (1, 2, 8)
    ]
    outgoing = jnp.where(hits[0], first, jnp.where(hits[1], second, third))
    extra = stepped(outgoing, sign)
    got = jnp.where(at >= PLANE, 1, 2)
    return extra, jnp.stack([jnp.where(hit, got, 0) for hit in hits]).astype(jnp.int32)


def pack_body(a_ref, b_ref, out_ref):
    out_ref[0, 0] = a_ref[...]
    out_ref[0, 1] = b_ref[...]


def pack_pair(a, b, parts):
    rows, cols = a.shape
    piece = pl.BlockSpec((rows, cols // parts), lambda i: (0, i))
    return pl.pallas_call(
        pack_body,
        out_shape=jax.ShapeDtypeStruct((parts, 2, rows, cols // parts), a.dtype),
        grid=(parts,),
        in_specs=[piece, piece],
        out_specs=pl.BlockSpec((1, 2, rows, cols // parts), lambda i: (i, 0, 0, 0)),
        name="pack_pair",
    )(a, b)


def pick_body(idx_ref, kv_ref, *rest):
    outs, sems = rest[:-1], rest[-1]
    copies = []
    for level in range(LEVELS):
        for slot in range(2):
            copies.append((kv_ref.at[idx_ref[level, slot]], outs[level].at[slot]))
    copies.append((kv_ref.at[:2], outs[LEVELS]))
    copies.append((kv_ref.at[2:], outs[LEVELS + 1]))
    copies = [pltpu.make_async_copy(src, dst, sems.at[n]) for n, (src, dst) in enumerate(copies)]
    for copy in copies:
        copy.start()
    for copy in copies:
        copy.wait()


def pick_blocks(idx, kv):
    shape = jax.ShapeDtypeStruct((2,) + kv.shape[1:], kv.dtype)
    return pl.pallas_call(
        pick_body,
        out_shape=[shape] * (LEVELS + 2),
        grid_spec=pltpu.PrefetchScalarGridSpec(
            num_scalar_prefetch=1,
            in_specs=[pl.BlockSpec(memory_space=pltpu.VMEM)],
            out_specs=[pl.BlockSpec(memory_space=pl.ANY)] * (LEVELS + 2),
            grid=(1,),
            scratch_shapes=[pltpu.SemaphoreType.DMA((2 * LEVELS + 2,))],
        ),
        name="pick_blocks",
    )(idx, kv)


def dot_nt(a, b):
    return lax.dot_general(a, b, (((1,), (1,)), ((), ())), preferred_element_type=jnp.float32)


def dot_nn(a, b):
    return lax.dot_general(a, b, (((1,), (0,)), ((), ())), preferred_element_type=jnp.float32)


def dot_tn(a, b):
    return lax.dot_general(a, b, (((0,), (0,)), ((), ())), preferred_element_type=jnp.float32)


def attend_body(
    span_ref, lists_ref, valid_ref, used_ref, from_ref,
    qd_ref, own_ref, prev0_ref, prev1_ref, far0_ref, far1_ref, far2_ref, extra_ref,
    att_ref, gq_ref, gown_ref, gprev0_ref, gprev1_ref, gfar0_ref, gfar1_ref, gfar2_ref,
    bias_ref, k_ref, v_ref,
):
    rows = 4 * BLOCK
    near = WINDOW + rows
    scale = HEAD_DIM ** -0.5

    @pl.when(pl.program_id(0) == 0)
    def _():
        first = span_ref[0] == 0
        i = lax.broadcasted_iota(jnp.int32, (rows, near), 0)
        j = lax.broadcasted_iota(jnp.int32, (rows, near), 1)
        low = jnp.where(first, WINDOW, 0)
        ok = (j > i) & (j <= i + WINDOW) & (j >= low)
        bias_ref[:, :near] = jnp.where(ok, 0.0, NEG)
        for b in range(4):
            for level in range(LEVELS):
                for slot in range(2):
                    hit = (valid_ref[b, level] > 0) & (lists_ref[b, level] == used_ref[level, slot])
                    value = jnp.where(hit, 0.0, NEG)
                    at = near + (level * 2 + slot) * BLOCK
                    bias_ref[b * BLOCK:(b + 1) * BLOCK, at:at + BLOCK] = jnp.full(
                        (BLOCK, BLOCK), value, jnp.float32
                    )

    at = 0
    for ref, blocks, source in (
        (prev0_ref, 2, 0), (prev1_ref, 2, None), (own_ref, 4, None),
        (far0_ref, 2, 1), (far1_ref, 2, 2), (far2_ref, 2, None),
    ):
        for b in range(blocks):
            for which, out in enumerate((k_ref, v_ref)):
                block = ref[b, which]
                if source is not None:
                    block = jnp.where(from_ref[source] == 1, extra_ref[b, which], block)
                out[at:at + BLOCK, :] = block
            at += BLOCK
    q = qd_ref[:, 0].reshape(rows, HEAD_DIM)
    d = qd_ref[:, 1].reshape(rows, HEAD_DIM)
    s = dot_nt(q, k_ref[...]) * scale + bias_ref[...]
    m = jnp.max(s, -1, keepdims=True)
    p = jnp.exp(s - m)
    total = jnp.sum(p, -1, keepdims=True)
    w = p * (1.0 / total)
    wb = w.astype(jnp.bfloat16)
    att = dot_nn(wb, v_ref[...]).astype(jnp.bfloat16)
    att_ref[...] = att.reshape(4, BLOCK, HEAD_DIM)
    delta = jnp.sum(d.astype(jnp.float32) * att.astype(jnp.float32), -1, keepdims=True)
    dp = dot_nt(d, v_ref[...])
    ds = (w * (dp - delta)).astype(jnp.bfloat16)
    gq_ref[...] = (dot_nn(ds, k_ref[...]) * scale).astype(jnp.bfloat16)
    gk = dot_tn(ds, q) * scale
    gv = dot_tn(wb, d)
    gown_ref[0] = gk[WINDOW:near]
    gown_ref[1] = gv[WINDOW:near]
    for a, ref in (
        (0, gprev0_ref), (2 * BLOCK, gprev1_ref),
        (near, gfar0_ref), (near + 2 * BLOCK, gfar1_ref), (near + 4 * BLOCK, gfar2_ref),
    ):
        ref[:, 0] = gk[a:a + 2 * BLOCK].astype(jnp.bfloat16).reshape(2, BLOCK, HEAD_DIM)
        ref[:, 1] = gv[a:a + 2 * BLOCK].astype(jnp.bfloat16).reshape(2, BLOCK, HEAD_DIM)


def attend(span, lists, valid, used, source, qd, own, prevs, fars, extra):
    cols = qd.shape[-1]
    heads = cols // HEAD_DIM
    rows = 4 * BLOCK
    keys = WINDOW + rows + 2 * LEVELS * BLOCK

    def piece(*lead):
        return pl.BlockSpec(lead + (HEAD_DIM,), lambda h, *_: (0,) * len(lead) + (h,))

    four, two = piece(4, 2, BLOCK), piece(2, 2, BLOCK)
    bf = jnp.bfloat16
    return pl.pallas_call(
        attend_body,
        out_shape=[
            jax.ShapeDtypeStruct((4, BLOCK, cols), bf),
            jax.ShapeDtypeStruct((rows, cols), bf),
            jax.ShapeDtypeStruct((2, rows, cols), jnp.float32),
        ] + [jax.ShapeDtypeStruct((2, 2, BLOCK, cols), bf)] * (LEVELS + 2),
        grid_spec=pltpu.PrefetchScalarGridSpec(
            num_scalar_prefetch=5,
            grid=(heads,),
            in_specs=[four, four] + [two] * (LEVELS + 3),
            out_specs=[piece(4, BLOCK), piece(rows), piece(2, rows)] + [two] * (LEVELS + 2),
            scratch_shapes=[
                pltpu.VMEM((rows, keys), jnp.float32),
                pltpu.VMEM((keys, HEAD_DIM), bf),
                pltpu.VMEM((keys, HEAD_DIM), bf),
            ],
        ),
        name="attend",
    )(span, lists, valid, used, source, qd, own, *prevs, *fars, extra)


def total_body(
    idx_ref, from_ref, gown_ref, gprev0_ref, gprev1_ref, gfar0_ref, gfar1_ref, gfar2_ref, extra_ref,
    gk_ref, gv_ref, acc_ref,
):
    def part(ref, slot, source):
        block = ref[slot].astype(jnp.float32)
        if source is not None:
            other = extra_ref[slot].astype(jnp.float32)
            own = from_ref[source]
            block = jnp.where(own == 0, block, jnp.where(own == 1, other, 0.0))
        return block

    for b in range(4):
        rows = slice(b * BLOCK, (b + 1) * BLOCK)
        acc_ref[b] = gown_ref[:, rows] + (part(gprev0_ref, b, 0) if b < 2 else part(gprev1_ref, b - 2, None))
    for level, (ref, source) in enumerate(((gfar0_ref, 1), (gfar1_ref, 2), (gfar2_ref, None))):
        for slot in range(2):
            at = idx_ref[level, slot]
            acc_ref[at] += part(ref, slot, source)
    for b in range(4):
        gk_ref[b * BLOCK:(b + 1) * BLOCK, :] = acc_ref[b, 0].astype(jnp.bfloat16)
        gv_ref[b * BLOCK:(b + 1) * BLOCK, :] = acc_ref[b, 1].astype(jnp.bfloat16)


def total(idx, source, gown, gprevs, gfars, extra):
    cols = gown.shape[-1]
    rows = 4 * BLOCK
    step = 256

    def piece(*lead):
        return pl.BlockSpec(lead + (step,), lambda h, *_: (0,) * len(lead) + (h,))

    out = jax.ShapeDtypeStruct((rows, cols), jnp.bfloat16)
    return pl.pallas_call(
        total_body,
        out_shape=[out, out],
        grid_spec=pltpu.PrefetchScalarGridSpec(
            num_scalar_prefetch=2,
            grid=(cols // step,),
            in_specs=[piece(2, rows)] + [piece(2, 2, BLOCK)] * (LEVELS + 3),
            out_specs=[piece(rows), piece(rows)],
            scratch_shapes=[pltpu.VMEM((4, 2, BLOCK, step), jnp.float32)],
        ),
        name="total",
    )(idx, source, gown, *gprevs, *gfars, extra)


def spread(x):
    return lax.all_to_all(x, "head", split_axis=0, concat_axis=0)


def per_device(q_tokens, k_tokens, v_tokens, grad_out, block_lists, block_valid):
    parts = lax.axis_size("head")
    span = lax.axis_index("seq").astype(jnp.int32).reshape(1)
    used = jnp.stack([jnp.min(block_lists, 0), jnp.max(block_lists, 0)], 1)
    kv = pack_pair(k_tokens, v_tokens, parts)
    asked = jnp.stack([passed(used[level], -2 * 4**level) for level in range(LEVELS)])
    own = spread(kv)
    qd, asked = lax.optimization_barrier((pack_pair(q_tokens, grad_out, parts), asked))
    *picked, half0, half1 = pick_blocks(asked, own)
    far1 = passed(picked[1], 8, True)
    far0 = passed(picked[0], 2, True)
    prev0 = passed(half0, 1, True)
    far2 = passed(picked[2], 32)
    prev1 = passed(half1, 1)
    extra, source = relayed(prev0, far0, far1, 1)
    qd = spread(qd)
    att, grad_q, gown, gprev0, gprev1, *gfars = attend(
        span, block_lists, block_valid, used, source, qd, own, (prev0, prev1), (far0, far1, far2), extra
    )
    back1 = passed(gfars[1], -8, True)
    back0 = passed(gfars[0], -2, True)
    bprev0 = passed(gprev0, -1, True)
    back2 = passed(gfars[2], -32)
    bprev1 = passed(gprev1, -1)
    extra, source = relayed(bprev0, back0, back1, -1)
    attended = spread(att).transpose(1, 0, 2).reshape(q_tokens.shape)
    grad_k, grad_v = total(asked, source, gown, (bprev0, bprev1), (back0, back1, back2), extra)
    return attended, grad_q, grad_k, grad_v


def solution(mesh):
    tokens = P(("seq", "head"), None)
    return jax.shard_map(
        per_device,
        mesh=mesh,
        in_specs=(tokens,) * 4 + (P("seq", None),) * 2,
        out_specs=(tokens,) + (P("seq", "head"),) * 3,
        check_vma=False,
    )
```

```python
import functools

import jax
import jax.numpy as jnp
from jax import lax
from jax.experimental import pallas as pl
from jax.experimental.pallas import tpu as pltpu
from jax.sharding import PartitionSpec as P


HEAD_DIM = 128
WINDOW = 256
BLOCK = 64
LEVELS = 3
NEG = -1e30


DETOURS = {1: {15: 0}, 2: {15: 1}, 8: {14: 6, 15: 7}}
PLANE = 16


def pairs_of(peers, by, detour):
    pairs = []
    for i in range(peers):
        if i + by < peers:
            to = i + by
            if detour and to // PLANE > i // PLANE:
                at = DETOURS[by].get(i % PLANE)
                to = to if at is None else i // PLANE * PLANE + at
            pairs.append((i, to))
    return pairs


def passed(shard, by, detour=False):
    peers = lax.axis_size("seq")
    pairs = pairs_of(peers, abs(by), detour)
    if by < 0:
        pairs = [(peers - 1 - i, peers - 1 - j) for i, j in pairs]
    return lax.ppermute(shard, "seq", pairs)


def stepped(shard, by):
    peers = lax.axis_size("seq")
    relays = list(DETOURS[abs(by)].values())
    pairs = [(i, i + PLANE) for i in range(peers - PLANE) if i % PLANE in relays]
    at = lax.axis_index("seq")
    if by < 0:
        pairs = [(peers - 1 - i, peers - 1 - j) for i, j in pairs]
        at = peers - 1 - at
    hit = functools.reduce(jnp.logical_or, [at % PLANE == v for v in relays])
    source = jnp.where(hit, jnp.where(at >= PLANE, 1, 2), 0).astype(jnp.int32)
    return lax.ppermute(shard, "seq", pairs), source


def pack_body(a_ref, b_ref, out_ref):
    out_ref[0, 0] = a_ref[...]
    out_ref[0, 1] = b_ref[...]


def pack_pair(a, b, parts):
    rows, cols = a.shape
    piece = pl.BlockSpec((rows, cols // parts), lambda i: (0, i))
    return pl.pallas_call(
        pack_body,
        out_shape=jax.ShapeDtypeStruct((parts, 2, rows, cols // parts), a.dtype),
        grid=(parts,),
        in_specs=[piece, piece],
        out_specs=pl.BlockSpec((1, 2, rows, cols // parts), lambda i: (i, 0, 0, 0)),
        name="pack_pair",
    )(a, b)


def pick_body(idx_ref, kv_ref, *rest):
    outs, sems = rest[:-1], rest[-1]
    copies = []
    for level in range(LEVELS):
        for slot in range(2):
            copies.append((kv_ref.at[idx_ref[level, slot]], outs[level].at[slot]))
    copies.append((kv_ref.at[:2], outs[LEVELS]))
    copies.append((kv_ref.at[2:], outs[LEVELS + 1]))
    copies = [pltpu.make_async_copy(src, dst, sems.at[n]) for n, (src, dst) in enumerate(copies)]
    for copy in copies:
        copy.start()
    for copy in copies:
        copy.wait()


def pick_blocks(idx, kv):
    shape = jax.ShapeDtypeStruct((2,) + kv.shape[1:], kv.dtype)
    return pl.pallas_call(
        pick_body,
        out_shape=[shape] * (LEVELS + 2),
        grid_spec=pltpu.PrefetchScalarGridSpec(
            num_scalar_prefetch=1,
            in_specs=[pl.BlockSpec(memory_space=pltpu.VMEM)],
            out_specs=[pl.BlockSpec(memory_space=pl.ANY)] * (LEVELS + 2),
            grid=(1,),
            scratch_shapes=[pltpu.SemaphoreType.DMA((2 * LEVELS + 2,))],
        ),
        name="pick_blocks",
    )(idx, kv)


def dot_nt(a, b):
    return lax.dot_general(a, b, (((1,), (1,)), ((), ())), preferred_element_type=jnp.float32)


def dot_nn(a, b):
    return lax.dot_general(a, b, (((1,), (0,)), ((), ())), preferred_element_type=jnp.float32)


def dot_tn(a, b):
    return lax.dot_general(a, b, (((0,), (0,)), ((), ())), preferred_element_type=jnp.float32)


PAIR = 2


def attend_body(
    span_ref, lists_ref, valid_ref, used_ref, from_ref,
    qd_ref, own_ref, prev0_ref, prev1_ref, far0_ref, far1_ref, far2_ref, *rest,
):
    extra_refs = rest[:3]
    (
    att_ref, ds_ref, wb_ref, gprev0_ref, gprev1_ref, gfar0_ref, gfar1_ref, gfar2_ref,
    bias_ref, k_ref, v_ref,
    ) = rest[3:]
    rows = 4 * BLOCK
    near = WINDOW + rows
    scale = HEAD_DIM ** -0.5
    bf = jnp.bfloat16

    @pl.when(pl.program_id(0) == 0)
    def _():
        first = span_ref[0] == 0
        i = lax.broadcasted_iota(jnp.int32, (rows, near), 0)
        j = lax.broadcasted_iota(jnp.int32, (rows, near), 1)
        low = jnp.where(first, WINDOW, 0)
        ok = (j > i) & (j <= i + WINDOW) & (j >= low)
        bias_ref[:, :near] = jnp.where(ok, 0.0, NEG)
        for b in range(4):
            for level in range(LEVELS):
                for slot in range(2):
                    hit = (valid_ref[b, level] > 0) & (lists_ref[b, level] == used_ref[level, slot])
                    value = jnp.where(hit, 0.0, NEG)
                    at = near + (level * 2 + slot) * BLOCK
                    bias_ref[b * BLOCK:(b + 1) * BLOCK, at:at + BLOCK] = jnp.full(
                        (BLOCK, BLOCK), value, jnp.float32
                    )

    heads = range(PAIR)
    lanes = [slice(n * HEAD_DIM, (n + 1) * HEAD_DIM) for n in heads]

    for n in heads:
        at = 0
        for ref, blocks, source in (
            (prev0_ref, 2, 0), (prev1_ref, 2, None), (own_ref, 4, None),
            (far0_ref, 2, 1), (far1_ref, 2, 2), (far2_ref, 2, None),
        ):
            for b in range(blocks):
                for which, out in enumerate((k_ref, v_ref)):
                    block = ref[b, which, :, lanes[n]]
                    if source is not None:
                        other = extra_refs[source][b, which, :, lanes[n]]
                        block = jnp.where(from_ref[source] == 1, other, block)
                    out[n, at:at + BLOCK, :] = block
                at += BLOCK
    q = [qd_ref[:, 0, :, lanes[n]].reshape(rows, HEAD_DIM) for n in heads]
    d = [qd_ref[:, 1, :, lanes[n]].reshape(rows, HEAD_DIM) for n in heads]
    s = [dot_nt(q[n], k_ref[n]) for n in heads]
    w, wb, dp = [None] * PAIR, [None] * PAIR, [None] * PAIR
    for n in heads:
        dp[n] = dot_nt(d[n], v_ref[n])
        t = s[n] * scale + bias_ref[...]
        p = jnp.exp(t - jnp.max(t, -1, keepdims=True))
        w[n] = p * (1.0 / jnp.sum(p, -1, keepdims=True))
        wb[n] = w[n].astype(bf)
    for n in heads:
        att = dot_nn(wb[n], v_ref[n]).astype(bf)
        att_ref[:, :, lanes[n]] = att.reshape(4, BLOCK, HEAD_DIM)
        delta = jnp.sum(d[n].astype(jnp.float32) * att.astype(jnp.float32), -1, keepdims=True)
        ds = (w[n] * (dp[n] - delta)).astype(bf)
        ds_ref[n] = ds
        wb_ref[n] = wb[n][:, WINDOW:near]
        for a, c, refs in (
            (0, WINDOW, (gprev0_ref, gprev1_ref)),
            (near, near + 2 * LEVELS * BLOCK, (gfar0_ref, gfar1_ref, gfar2_ref)),
        ):
            gv = dot_tn(wb[n][:, a:c], d[n])
            gk = dot_tn(ds[:, a:c], q[n]) * scale
            for part, ref in enumerate(refs):
                at = slice(2 * part * BLOCK, 2 * (part + 1) * BLOCK)
                ref[:, 0, :, lanes[n]] = gk[at].astype(bf).reshape(2, BLOCK, HEAD_DIM)
                ref[:, 1, :, lanes[n]] = gv[at].astype(bf).reshape(2, BLOCK, HEAD_DIM)


def attend(span, lists, valid, used, source, qd, own, prevs, fars, extras):
    cols = qd.shape[-1]
    step = PAIR * HEAD_DIM
    rows = 4 * BLOCK
    keys = WINDOW + rows + 2 * LEVELS * BLOCK

    def piece(*lead):
        return pl.BlockSpec(lead + (step,), lambda h, *_: (0,) * len(lead) + (h,))

    def when_sent(n):
        return pl.BlockSpec(
            (2, 2, BLOCK, step), lambda h, a, b, c, d, source: (0, 0, 0, jnp.where(source[n] == 1, h, 0))
        )

    def per_head(width):
        return pl.BlockSpec((PAIR, rows, width), lambda h, *_: (h, 0, 0))

    four, two = piece(4, 2, BLOCK), piece(2, 2, BLOCK)
    bf = jnp.bfloat16
    return pl.pallas_call(
        attend_body,
        out_shape=[
            jax.ShapeDtypeStruct((4, BLOCK, cols), bf),
            jax.ShapeDtypeStruct((cols // HEAD_DIM, rows, keys), bf),
            jax.ShapeDtypeStruct((cols // HEAD_DIM, rows, rows), bf),
        ] + [jax.ShapeDtypeStruct((2, 2, BLOCK, cols), bf)] * (LEVELS + 2),
        grid_spec=pltpu.PrefetchScalarGridSpec(
            num_scalar_prefetch=5,
            grid=(cols // step,),
            in_specs=[four, four] + [two] * (LEVELS + 2) + [when_sent(n) for n in range(3)],
            out_specs=[piece(4, BLOCK), per_head(keys), per_head(rows)] + [two] * (LEVELS + 2),
            scratch_shapes=[
                pltpu.VMEM((rows, keys), jnp.float32),
                pltpu.VMEM((PAIR, keys, HEAD_DIM), bf),
                pltpu.VMEM((PAIR, keys, HEAD_DIM), bf),
            ],
        ),
        name="attend",
    )(span, lists, valid, used, source, qd, own, *prevs, *fars, *extras)


def own_body(
    from_ref, qd_ref, own_ref, prev0_ref, prev1_ref, far0_ref, far1_ref, far2_ref, *rest,
):
    extra_refs, (ds_ref, wb_ref, gq_ref, gown_ref, k_ref) = rest[:3], rest[3:]
    rows = 4 * BLOCK
    near = WINDOW + rows
    scale = HEAD_DIM ** -0.5
    for n in range(PAIR):
        lanes = slice(n * HEAD_DIM, (n + 1) * HEAD_DIM)
        at = 0
        for ref, blocks, source in (
            (prev0_ref, 2, 0), (prev1_ref, 2, None), (own_ref, 4, None),
            (far0_ref, 2, 1), (far1_ref, 2, 2), (far2_ref, 2, None),
        ):
            for b in range(blocks):
                block = ref[b, 0, :, lanes]
                if source is not None:
                    block = jnp.where(from_ref[source] == 1, extra_refs[source][b, 0, :, lanes], block)
                k_ref[n, at:at + BLOCK, :] = block
                at += BLOCK
        q = qd_ref[:, 0, :, lanes].reshape(rows, HEAD_DIM)
        d = qd_ref[:, 1, :, lanes].reshape(rows, HEAD_DIM)
        ds = ds_ref[n]
        gq_ref[:, lanes] = (dot_nn(ds, k_ref[n]) * scale).astype(jnp.bfloat16)
        gown_ref[0, :, lanes] = dot_tn(ds[:, WINDOW:near], q) * scale
        gown_ref[1, :, lanes] = dot_tn(wb_ref[n], d)


def own_grads(source, qd, own, prevs, fars, extras, ds, wb):
    cols = qd.shape[-1]
    step = PAIR * HEAD_DIM
    rows = 4 * BLOCK
    keys = ds.shape[-1]

    def piece(*lead):
        return pl.BlockSpec(lead + (step,), lambda h, *_: (0,) * len(lead) + (h,))

    def keys_of(blocks):
        return pl.BlockSpec((blocks, 1, BLOCK, step), lambda h, *_: (0, 0, 0, h))

    def per_head(width):
        return pl.BlockSpec((PAIR, rows, width), lambda h, *_: (h, 0, 0))

    return pl.pallas_call(
        own_body,
        out_shape=[
            jax.ShapeDtypeStruct((rows, cols), jnp.bfloat16),
            jax.ShapeDtypeStruct((2, rows, cols), jnp.float32),
        ],
        grid_spec=pltpu.PrefetchScalarGridSpec(
            num_scalar_prefetch=1,
            grid=(cols // step,),
            in_specs=[piece(4, 2, BLOCK), keys_of(4)] + [keys_of(2)] * (LEVELS + 5) + [per_head(keys), per_head(rows)],
            out_specs=[piece(rows), piece(2, rows)],
            scratch_shapes=[pltpu.VMEM((PAIR, keys, HEAD_DIM), jnp.bfloat16)],
        ),
        name="own_grads",
    )(source, qd, own, *prevs, *fars, *extras, ds, wb)


def total_body(
    idx_ref, from_ref, gown_ref, gprev0_ref, gprev1_ref, gfar0_ref, gfar1_ref, gfar2_ref,
    extra0_ref, extra1_ref, extra2_ref, gk_ref, gv_ref, acc_ref,
):
    extra_refs = (extra0_ref, extra1_ref, extra2_ref)

    def part(ref, slot, source):
        block = ref[slot].astype(jnp.float32)
        if source is not None:
            other = extra_refs[source][slot].astype(jnp.float32)
            own = from_ref[source]
            block = jnp.where(own == 0, block, jnp.where(own == 1, other, 0.0))
        return block

    for b in range(4):
        rows = slice(b * BLOCK, (b + 1) * BLOCK)
        acc_ref[b] = gown_ref[:, rows] + (part(gprev0_ref, b, 0) if b < 2 else part(gprev1_ref, b - 2, None))
    for level, (ref, source) in enumerate(((gfar0_ref, 1), (gfar1_ref, 2), (gfar2_ref, None))):
        for slot in range(2):
            at = idx_ref[level, slot]
            acc_ref[at] += part(ref, slot, source)
    for b in range(4):
        gk_ref[b * BLOCK:(b + 1) * BLOCK, :] = acc_ref[b, 0].astype(jnp.bfloat16)
        gv_ref[b * BLOCK:(b + 1) * BLOCK, :] = acc_ref[b, 1].astype(jnp.bfloat16)


def total(idx, source, gown, gprevs, gfars, extras):
    cols = gown.shape[-1]
    rows = 4 * BLOCK
    step = 512

    def piece(*lead):
        return pl.BlockSpec(lead + (step,), lambda h, *_: (0,) * len(lead) + (h,))

    def when_sent(n):
        return pl.BlockSpec((2, 2, BLOCK, step), lambda h, idx, source: (0, 0, 0, jnp.where(source[n] == 1, h, 0)))

    out = jax.ShapeDtypeStruct((rows, cols), jnp.bfloat16)
    return pl.pallas_call(
        total_body,
        out_shape=[out, out],
        grid_spec=pltpu.PrefetchScalarGridSpec(
            num_scalar_prefetch=2,
            grid=(cols // step,),
            in_specs=[piece(2, rows)] + [piece(2, 2, BLOCK)] * (LEVELS + 2) + [when_sent(n) for n in range(3)],
            out_specs=[piece(rows), piece(rows)],
            scratch_shapes=[pltpu.VMEM((4, 2, BLOCK, step), jnp.float32)],
        ),
        name="total",
    )(idx, source, gown, *gprevs, *gfars, *extras)


def spread(x):
    return lax.all_to_all(x, "head", split_axis=0, concat_axis=0)


def second_steps(sign, *shards):
    pieces = [stepped(shard, sign * by) for by, shard in zip((1, 2, 8), shards)]
    return [piece for piece, _ in pieces], jnp.stack([source for _, source in pieces])


def per_device(q_tokens, k_tokens, v_tokens, grad_out, block_lists, block_valid):
    parts = lax.axis_size("head")
    span = lax.axis_index("seq").astype(jnp.int32).reshape(1)
    used = jnp.stack([jnp.min(block_lists, 0), jnp.max(block_lists, 0)], 1)
    kv = pack_pair(k_tokens, v_tokens, parts)
    asked = jnp.stack([passed(used[level], -2 * 4**level) for level in range(LEVELS)])
    own = spread(kv)
    qd, asked = lax.optimization_barrier((pack_pair(q_tokens, grad_out, parts), asked))
    *picked, half0, half1 = pick_blocks(asked, own)
    qd = spread(qd)
    far0 = passed(picked[0], 2, True)
    prev0 = passed(half0, 1, True)
    far1 = passed(picked[1], 8, True)
    far2 = passed(picked[2], 32)
    prev1 = passed(half1, 1)
    extras, source = second_steps(1, prev0, far0, far1)
    att, ds, wb, gprev0, gprev1, *gfars = attend(
        span, block_lists, block_valid, used, source, qd, own, (prev0, prev1), (far0, far1, far2), extras
    )
    back0 = passed(gfars[0], -2, True)
    bprev0 = passed(gprev0, -1, True)
    back1 = passed(gfars[1], -8, True)
    back2 = passed(gfars[2], -32)
    bprev1 = passed(gprev1, -1)
    bextras, bsource = second_steps(-1, bprev0, back0, back1)
    att = spread(att)
    grad_q, gown = own_grads(source, qd, own, (prev0, prev1), (far0, far1, far2), extras, ds, wb)
    attended = att.transpose(1, 0, 2).reshape(q_tokens.shape)
    grad_k, grad_v = total(asked, bsource, gown, (bprev0, bprev1), (back0, back1, back2), bextras)
    return attended, grad_q, grad_k, grad_v


def solution(mesh):
    tokens = P(("seq", "head"), None)
    return jax.shard_map(
        per_device,
        mesh=mesh,
        in_specs=(tokens,) * 4 + (P("seq", None),) * 2,
        out_specs=(tokens,) + (P("seq", "head"),) * 3,
        check_vma=False,
    )
```
